32 devices in a mesh: ctx: 8 (over z, y), fsdp: 4 (over x, core).
Axes of the slice: x: 2, y: 2, z: 4, core: 2. Of those that a mesh axis runs over, the one named last changes fastest.
Arguments:
- hidden: bfloat16 [4096, 4096], P('ctx', 'fsdp'), may hold values from -6 to 6
- w_in: bfloat16 [768, 4096], P('ctx', 'fsdp'), may hold values from -1.25 to 1.25
- decay: float32 [4, 4096], P(None, 'ctx'), may hold values from 0.999 to 1
- norm_gain: float32 [256], replicated, may hold values from 0.1 to 1.9
- w_out: bfloat16 [256, 4096], P('ctx', 'fsdp'), may hold values from -0.75 to 0.75
- grad_out: bfloat16 [4096, 4096], P('ctx', 'fsdp'), may hold values from -6 to 6
Outputs:
- grad_hidden: bfloat16 [4096, 4096], P('ctx', 'fsdp')
- grad_w_in: float32 [768, 4096], P('ctx', 'fsdp')
- grad_w_out: float32 [256, 4096], P('ctx', 'fsdp')
The draws below stay inside these ranges and needn't reach their ends.
All inputs are finite; a program needn't handle non-finite values.
Results may differ from the reference program's by a relative error of at most 0.0075.
Values may be sent and summed in bfloat16 or wider, within the bound.
A program may use at most 128 MiB of HBM per device.

```python
import math
import jax
import jax.numpy as jnp
from jax import lax

D = 4096
H = 4
P_SIZE = 64
N = 128
TOK_DEV = 512
HP = 256
CIN = 768
TOKENS = 4096


def draw_w_in(key, part):
    first, second = jax.random.split(key)
    scales = jnp.exp(jax.random.uniform(first, (CIN, 1), jnp.float32, math.log(0.1), math.log(10.0)))
    ramp = jnp.arange(D, dtype=jnp.float32)[None, :] / (D - 1)
    entries = jnp.clip(jax.random.normal(second, (CIN, D), jnp.float32), -4.0, 4.0)
    profile = jnp.exp(math.log(0.6) + ramp * (math.log(1.8) - math.log(0.6)))
    return (entries * scales * profile / math.sqrt(D)).astype(jnp.bfloat16)


def draw_w_out(key, part):
    first, second = jax.random.split(key)
    scales = jnp.exp(jax.random.uniform(first, (1, D), jnp.float32, math.log(0.3), math.log(3.0)))
    entries = jnp.clip(jax.random.normal(second, (HP, D), jnp.float32), -4.0, 4.0)
    return (entries * scales / math.sqrt(HP)).astype(jnp.bfloat16)


def draw_decay(key, part):
    first, second, third, fourth = jax.random.split(key, 4)
    order = jax.random.permutation(first, H)
    slow_base = jnp.minimum(jax.random.uniform(second, (H, 1), jnp.float32, 0.2, 0.8) * math.log(10.0) / TOKENS, 0.00025)
    fast_base = jnp.exp(jax.random.uniform(third, (H, 1), jnp.float32, math.log(6e-05), math.log(0.00025)))
    rates = jnp.where(order[:, None] < H // 2, slow_base, fast_base)
    blocks = TOKENS // TOK_DEV
    block_factor = jnp.exp(jax.random.uniform(fourth, (H, blocks, 1), jnp.float32, math.log(0.25), math.log(4.0)))
    jitter = jnp.broadcast_to(block_factor, (H, blocks, TOK_DEV)).reshape(H, TOKENS)
    per_token = jnp.minimum(rates * jitter, 0.001)
    return jnp.exp(-per_token).astype(jnp.float32)


def block_levels(own_key, extent, cuts, low, top_value):
    loudness = 1.0
    for axis_at, parts in cuts:
        heights = jax.random.uniform(jax.random.fold_in(jax.random.fold_in(own_key, 6), axis_at), (parts,), jnp.float32, low / len(cuts), top_value / len(cuts))
        loudness = loudness * jnp.repeat(jnp.exp(heights), extent[axis_at] // parts).reshape((-1,) + (1,) * (len(extent) - 1 - axis_at))
    return loudness


def gaussian(own_key, extent, width, reach, cuts=(), kind=jnp.bfloat16):
    drawn = width * jax.random.normal(own_key, extent, jnp.float32)
    if cuts:
        drawn = drawn * block_levels(own_key, extent, cuts, -0.22, 0.18)
    return jnp.clip(drawn, -reach, reach).astype(kind)


def setup_inputs(seed: int = 0) -> dict:
    key_list = jax.random.split(jax.random.key(seed), 7)
    hidden = gaussian(key_list[0], (TOKENS, D), 1.0, 6.0, ((0, 8), (1, 4)))
    w_in = draw_w_in(jax.random.fold_in(key_list[6], 71), 0)
    decay = draw_decay(jax.random.fold_in(key_list[6], 71), 0)
    norm_gain = jnp.clip(1.0 + 0.18 * jax.random.normal(key_list[3], (HP,), jnp.float32), 0.1, 1.9)
    w_out = draw_w_out(jax.random.fold_in(key_list[6], 71), 0)
    grad_out = gaussian(key_list[5], (TOKENS, D), 1.0, 6.0, ((0, 8), (1, 4)))
    return {"hidden": hidden, "w_in": w_in, "decay": decay, "norm_gain": norm_gain, "w_out": w_out, "grad_out": grad_out}


highest = lax.Precision.HIGHEST
clip_output = 10.0

def split_columns(projection):
    return (projection[:, :HP], projection[:, HP:2 * HP], projection[:, 2 * HP:2 * HP + N], projection[:, 2 * HP + N:])

def intra_block(x_part, b_part, c_part, log_decay):
    length = x_part.shape[0]
    cum_decay = jnp.cumsum(log_decay, axis=1)
    x_heads = x_part.reshape(length, H, P_SIZE)
    causal = jnp.arange(length)[:, None] >= jnp.arange(length)[None, :]
    gaps = jnp.where(causal[None], cum_decay[:, :, None] - cum_decay[:, None, :], 0.0)
    weights = jnp.where(causal[None], jnp.exp(gaps), 0.0)
    scores = jnp.dot(c_part, b_part.T, precision=highest)
    mixed = weights * scores[None]
    y_intra = jnp.einsum('hts,shp->thp', mixed, x_heads, precision=highest).reshape(length, H * P_SIZE)
    tail = jnp.exp(cum_decay[:, -1:] - cum_decay)
    weighted = x_heads * tail.T[:, :, None]
    state_part = jnp.einsum('shp,sn->hpn', weighted, b_part, precision=highest)
    return (y_intra, state_part, cum_decay)

def finish_block(gate_part, y_intra, c_part, start_state, cum_decay, norm_gain):
    length = c_part.shape[0]
    carried = jnp.einsum('hpn,tn->thp', start_state, c_part, precision=highest)
    carried = carried * jnp.exp(cum_decay).T[:, :, None]
    y_full = y_intra + carried.reshape(length, H * P_SIZE)
    gated = y_full * jax.nn.silu(gate_part)
    factor = lax.rsqrt(lax.optimization_barrier(jnp.mean(gated * gated, axis=-1, keepdims=True)) + 1e-05)
    return gated * factor * norm_gain

def mixer(projection, log_decay, norm_gain):
    blocks = TOKENS // TOK_DEV
    stacked = projection.reshape(blocks, TOK_DEV, CIN)
    decays = log_decay.reshape(H, blocks, TOK_DEV).transpose(1, 0, 2)

    def advance(start_state, inputs):
        block, block_decay = inputs
        gate_part, x_part, b_part, c_part = split_columns(block)
        y_intra, state_part, cum_decay = intra_block(x_part, b_part, c_part, block_decay)
        normed = finish_block(gate_part, y_intra, c_part, start_state, cum_decay, norm_gain)
        end_state = jnp.exp(cum_decay[:, -1])[:, None, None] * start_state + state_part
        return (end_state, normed)
    _, normed = lax.scan(advance, jnp.zeros((H, P_SIZE, N), jnp.float32), (stacked, decays))
    return normed.reshape(TOKENS, HP)

def reference(hidden, w_in, decay, norm_gain, w_out, grad_out):
    clip_input = math.sqrt(D)
    projection = jnp.dot(hidden, w_in.T, preferred_element_type=jnp.float32)
    grad_normed = jnp.dot(grad_out, w_out.T, preferred_element_type=jnp.float32)
    log_decay = jnp.log(decay)
    normed, pullback = jax.vjp(lambda value: mixer(value, log_decay, norm_gain), projection)
    grad_projection = pullback(grad_normed)[0].astype(jnp.bfloat16)
    normed_rounded = normed.astype(jnp.bfloat16)
    grad_hidden = jnp.dot(grad_projection, w_in, preferred_element_type=jnp.float32).astype(jnp.bfloat16)
    root_tokens = math.sqrt(TOKENS)
    raw_in = jnp.dot(grad_projection.T, hidden, preferred_element_type=jnp.float32) / root_tokens
    raw_out = jnp.dot(normed_rounded.T, grad_out, preferred_element_type=jnp.float32) / root_tokens
    weight_in = jnp.sqrt(lax.optimization_barrier(jnp.sum(jnp.square(w_in.astype(jnp.float32)), axis=1)))
    norm_in = jnp.sqrt(lax.optimization_barrier(jnp.sum(raw_in * raw_in, axis=1)))
    factor_in = jnp.minimum(1.0, clip_input * jnp.maximum(weight_in, 0.001) / jnp.maximum(norm_in, 1e-06))
    weight_out = jnp.sqrt(lax.optimization_barrier(jnp.sum(jnp.square(w_out.astype(jnp.float32)), axis=0)))
    norm_out = jnp.sqrt(lax.optimization_barrier(jnp.sum(raw_out * raw_out, axis=0)))
    factor_out = jnp.minimum(1.0, clip_output * jnp.maximum(weight_out, 0.001) / jnp.maximum(norm_out, 1e-06))
    return (grad_hidden, raw_in * factor_in[:, None], raw_out * factor_out[None, :])
```

```python
import functools
import math

import jax
import jax.numpy as jnp
from jax import lax
from jax.experimental import pallas as pl
from jax.experimental.pallas import tpu as pltpu
from jax.sharding import PartitionSpec as P

D = 4096
H = 4
P_SIZE = 64
N = 128
HP = 256


highest = lax.Precision.HIGHEST
clip_output = 10.0


def prefix(x, axis, combine, identity):
    count, index = (lax.axis_size(axis), lax.axis_index(axis))
    everything = jax.tree.map(lambda part: lax.all_gather(part, axis), x)
    start = jax.tree.map(
        lambda part, zero: jnp.broadcast_to(jnp.asarray(zero, part.dtype), part.shape), x, identity
    )

    def step(k, before):
        reached = k < index
        new = combine(before, jax.tree.map(lambda part: part[k], everything))
        return jax.tree.map(lambda a, b: jnp.where(reached, a, b), new, before)

    return lax.fori_loop(0, count, step, start)


def entering(x, axis, join, neutral):
    count = lax.axis_size(axis)
    place = lax.axis_index(axis)
    ahead = count - 1 - place
    gathered = jax.tree.map(
        lambda a, kind: lax.all_gather(a.astype(kind), axis),
        x,
        jax.tree.map(lambda a: jnp.bfloat16 if a.dtype == jnp.float32 else a.dtype, x),
    )
    state = jax.tree.map(lambda a, e: jnp.zeros_like(a) + jnp.asarray(e, a.dtype), x, neutral)

    def one(step, state):
        source = count - 1 - step
        return join(
            state,
            jax.tree.map(
                lambda a, own: lax.dynamic_index_in_dim(a, source, 0, False).astype(own.dtype),
                gathered,
                x,
            ),
        )

    return lax.fori_loop(0, ahead, one, state)


def split_columns(projection):
    return (
        projection[:, :HP],
        projection[:, HP : 2 * HP],
        projection[:, 2 * HP : 2 * HP + N],
        projection[:, 2 * HP + N :],
    )


def intra_block(x_part, b_part, c_part, log_decay):
    length = x_part.shape[0]
    cum_decay = jnp.cumsum(log_decay, axis=1)
    x_heads = x_part.reshape(length, H, P_SIZE)
    causal = jnp.arange(length)[:, None] >= jnp.arange(length)[None, :]
    gaps = jnp.where(causal[None], cum_decay[:, :, None] - cum_decay[:, None, :], 0.0)
    weights = jnp.where(causal[None], jnp.exp(gaps), 0.0)
    scores = jnp.dot(c_part, b_part.T, precision=highest)
    mixed = weights * scores[None]
    y_intra = jnp.einsum("hts,shp->thp", mixed, x_heads, precision=highest).reshape(
        length, H * P_SIZE
    )
    tail = jnp.exp(cum_decay[:, -1:] - cum_decay)
    weighted = x_heads * tail.T[:, :, None]
    state_part = jnp.einsum("shp,sn->hpn", weighted, b_part, precision=highest)
    return (y_intra, state_part, cum_decay)


def finish_block(gate_part, y_intra, c_part, start_state, cum_decay, norm_gain):
    length = c_part.shape[0]
    carried = jnp.einsum("hpn,tn->thp", start_state, c_part, precision=highest)
    carried = carried * jnp.exp(cum_decay).T[:, :, None]
    y_full = y_intra + carried.reshape(length, H * P_SIZE)
    gated = y_full * jax.nn.silu(gate_part)
    factor = lax.rsqrt(jnp.mean(gated * gated, axis=-1, keepdims=True) + 1e-05)
    return gated * factor * norm_gain


def carry_states(earlier, later):
    return (earlier[0] * later[0], later[0] * earlier[1] + later[1])


def carry_adjoint(earlier, later):
    return (earlier[0] * later[0], later[1] + later[0] * earlier[1])


def local(hidden, w_in, decay, norm_gain, w_out, grad_out):
    clip_input = math.sqrt(D)
    tok_rows = hidden.shape[0]
    root_tokens = math.sqrt(tok_rows * lax.axis_size("ctx"))
    contract_last = (((1,), (1,)), ((), ()))
    contract_first = (((0,), (0,)), ((), ()))
    partial_proj = lax.dot_general(
        hidden,
        lax.all_gather(w_in, "ctx", axis=0, tiled=True),
        contract_last,
        preferred_element_type=jnp.float32,
    )
    slab_out = lax.all_gather(w_out, "ctx", axis=0, tiled=True)
    partial_grad = lax.dot_general(
        grad_out, slab_out, contract_last, preferred_element_type=jnp.float32
    )
    projection, grad_normed = lax.psum((partial_proj, partial_grad), "fsdp")
    log_decay = jnp.log(decay)
    gate_part, x_part, b_part, c_part = split_columns(projection)

    def intra_only(x_value, b_value, c_value):
        return intra_block(x_value, b_value, c_value, log_decay)

    (y_intra, state_part, cum_decay), intra_pull = jax.vjp(intra_only, x_part, b_part, c_part)
    decay_total = jnp.exp(cum_decay[:, -1])[:, None, None]
    identity = (jnp.ones_like(decay_total), jnp.zeros_like(state_part))
    _, start_state = prefix((decay_total, state_part), "ctx", carry_states, identity)

    def finish_only(gate_value, intra_value, c_value, state_value):
        return finish_block(gate_value, intra_value, c_value, state_value, cum_decay, norm_gain)

    normed, finish_pull = jax.vjp(finish_only, gate_part, y_intra, c_part, start_state)
    grad_gate, grad_intra, grad_c_late, grad_start = finish_pull(grad_normed)
    _, grad_end = entering((decay_total, grad_start), "ctx", carry_adjoint, identity)
    grad_x, grad_b, grad_c_early = intra_pull((grad_intra, grad_end, jnp.zeros_like(cum_decay)))
    grad_projection = jnp.concatenate(
        [grad_gate, grad_x, grad_b, grad_c_early + grad_c_late], axis=1
    ).astype(jnp.bfloat16)
    columns = grad_projection
    grad_hidden = jnp.dot(
        columns, lax.all_gather(w_in, "ctx", axis=0, tiled=True), preferred_element_type=jnp.float32
    )
    columns = grad_projection
    raw_in = (
        lax.psum_scatter(
            lax.dot_general(columns, hidden, contract_first, preferred_element_type=jnp.float32),
            "ctx",
            scatter_dimension=0,
            tiled=True,
        )
        / root_tokens
    )
    weight_square = jnp.sum(jnp.square(w_in.astype(jnp.float32)), axis=1)
    weight_in, grad_in = lax.psum((weight_square, jnp.sum(raw_in * raw_in, axis=1)), "fsdp")
    factor_in = jnp.minimum(
        1.0,
        clip_input
        * jnp.maximum(jnp.sqrt(weight_in), 0.001)
        / jnp.maximum(jnp.sqrt(grad_in), 1e-06),
    )
    normed_rounded = normed.astype(jnp.bfloat16)
    weight_out = jnp.sqrt(jnp.sum(jnp.square(slab_out.astype(jnp.float32)), axis=0))
    raw_out = (
        lax.psum_scatter(
            lax.dot_general(
                normed_rounded, grad_out, contract_first, preferred_element_type=jnp.float32
            ),
            "ctx",
            scatter_dimension=0,
            tiled=True,
        )
        / root_tokens
    )
    grad_square = lax.psum(jnp.sum(raw_out * raw_out, axis=0), "ctx")
    factor_out = jnp.minimum(
        1.0,
        clip_output * jnp.maximum(weight_out, 0.001) / jnp.maximum(jnp.sqrt(grad_square), 1e-06),
    )
    return (
        grad_hidden.astype(jnp.bfloat16),
        raw_in * factor_in[:, None],
        raw_out * factor_out[None, :],
    )


NN = (((1,), (0,)), ((), ()))
NT = (((1,), (1,)), ((), ()))
TN = (((0,), (0,)), ((), ()))
MESH = pl.DeviceIdType.MESH
f32 = jnp.float32
bf16 = jnp.bfloat16
EPS = 1e-05
PARTS = 4


def split(a):
    hi = a.astype(bf16)
    return hi, (a - hi.astype(f32)).astype(bf16)


def dot1(a, b, dims):
    return lax.dot_general(a, b, dims, preferred_element_type=f32)


def dot3(a, b, dims):
    return dot1(a[0], b[0], dims) + (dot1(a[0], b[1], dims) + dot1(a[1], b[0], dims))


def transposed(pair):
    return pair[0].T, pair[1].T


def fused(
    n, fs, root_tokens, clip_input,
    hid_ref, win_ref, dec_ref, gain_ref, wout_ref, gout_ref,
    gh_ref, gwi_ref, gwo_ref,
    hidT, goutT, wi_all, wo_all, pT, core_in, x_out, x_in,
    e_ref, st_out, st_all, s0_ref, ad_out, ad_all, g_ref,
    ro, ob1, ob1r, ob2, ob2r, gp, ri, ib1, ib1r, ib2, ib2r,
    nin_out, nin_all, nout_out, nout_all,
    g_send, g_recv, p_send, p_recv, s_send, s_recv, o_send, o_recv, i_send, i_recv,
    n_send, n_recv, tmp, c_in,
):
    c = lax.axis_index("ctx")
    f = lax.axis_index("fsdp")
    outer = n // 2
    z, y = c // 2, lax.rem(c, 2)
    yn = c + 1 - 2 * y
    core = lax.rem(f, 2)
    fcore = f + 1 - 2 * core
    fx = lax.rem(f + fs // 2, fs)
    rows_in, d = win_ref.shape
    rows_out = wout_ref.shape[0]
    tok = hid_ref.shape[0]
    cin, hp = rows_in * n, rows_out * n
    nst = (cin - 2 * hp) // 2
    hpf = hp // fs

    def copy(src, dst, ssem, rsem, dev):
        return pltpu.make_async_remote_copy(
            src_ref=src, dst_ref=dst, send_sem=ssem, recv_sem=rsem,
            device_id=dev, device_id_type=MESH)

    sent = []

    def go(*args):
        made = copy(*args)
        made.start()
        sent.append(made)
        return made

    barrier = pltpu.get_barrier_semaphore()
    for k in range(1, n):
        pl.semaphore_signal(barrier, inc=1, device_id=(lax.rem(c + k, n), f), device_id_type=MESH)
    for k in range(1, fs):
        pl.semaphore_signal(barrier, inc=1, device_id=(c, lax.rem(f + k, fs)), device_id_type=MESH)
    pl.semaphore_wait(barrier, n + fs - 2)

    both = ((win_ref, wi_all), (wout_ref, wo_all))
    for a, (src, dst) in enumerate(both):
        go(src, dst.at[c], g_send.at[a, 0], g_recv.at[a, c], (yn, f))
    order = [1, outer - 1] + list(range(2, outer - 1))
    for k in order:
        peer = lax.rem(z + k, outer) * 2 + y
        for a, (src, dst) in enumerate(both):
            go(src, dst.at[c], g_send.at[a, k], g_recv.at[a, c], (peer, f))
    wi_all[c] = win_ref[...]
    wo_all[c] = wout_ref[...]
    hidT[...] = hid_ref[...].T
    goutT[...] = gout_ref[...].T

    decay = dec_ref[...]
    lane = lax.broadcasted_iota(jnp.int32, decay.shape, 1)
    shift = 1
    while shift < tok:
        decay = decay * jnp.where(lane >= shift, pltpu.roll(decay, shift, 1), 1.0)
        shift *= 2
    heads = decay.shape[0]
    for h in range(heads):
        e_ref[h * (hp // heads) : (h + 1) * (hp // heads), :] = jnp.broadcast_to(
            decay[h : h + 1], (hp // heads, tok))

    def project(s):
        pT[pl.ds(pl.multiple_of(s * rows_in, 8), rows_in), :] = dot1(wi_all[s], hidT[...], NN)
        pT[pl.ds(pl.multiple_of(cin + s * rows_out, 8), rows_out), :] = dot1(
            wo_all[s], goutT[...], NN)

    project(c)
    for k in order:
        s = lax.rem(z + outer - k, outer) * 2 + y
        for a, (src, dst) in enumerate(both):
            copy(src, dst.at[s], g_send.at[a, k], g_recv.at[a, s], (yn, f)).wait_recv()
            go(dst.at[s], dst.at[s], g_send.at[a, outer + k], g_recv.at[a, s], (yn, f))
        project(s)
    for k in [0] + order:
        s = lax.rem(z + outer - k, outer) * 2 + 1 - y
        for a, (src, dst) in enumerate(both):
            copy(src, dst.at[s], g_send.at[a, 0], g_recv.at[a, s], (yn, f)).wait_recv()
        project(s)

    half = (cin + hp) // 2
    size = half // PARTS
    first = []
    for j in range(PARTS):
        part = pl.ds(pl.multiple_of((1 - core) * half + j * size, 8), size)
        first.append(copy(pT.at[part], core_in.at[j], p_send.at[0, j], p_recv.at[0, j], (c, fcore)))
        first[j].start()
    mine = [pl.ds(pl.multiple_of(core * half + j * size, 8), size) for j in range(PARTS)]
    for j in range(PARTS):
        copy(core_in.at[j], core_in.at[j], p_send.at[0, j], p_recv.at[0, j], (c, fcore)).wait_recv()
        total = pT[mine[j], :] + core_in[j]
        pT[mine[j], :] = total
        x_out[j] = total.astype(bf16)
        go(x_out.at[j], x_in.at[j], p_send.at[1, j], p_recv.at[1, j], (c, fx))
    for j in range(PARTS):
        copy(x_out.at[j], x_in.at[j], p_send.at[1, j], p_recv.at[1, j], (c, fx)).wait_recv()
        pT[mine[j], :] = pT[mine[j], :] + x_in[j].astype(f32)
        go(pT.at[mine[j]], c_in.at[j], p_send.at[2, j], p_recv.at[2, j], (c, fcore))
    for j in range(PARTS):
        first[j].wait_send()
    for j in range(PARTS):
        part = pl.ds(pl.multiple_of((1 - core) * half + j * size, 8), size)
        copy(c_in.at[j], c_in.at[j], p_send.at[2, j], p_recv.at[2, j], (c, fcore)).wait_recv()
        pT[part, :] = c_in[j]

    e = e_ref[...]
    einv = 1.0 / e
    eend = e[:, tok - 1 : tok]
    gate = pT[:hp, :]
    xs = pT[hp : 2 * hp, :] * einv
    bT = pT[2 * hp : 2 * hp + nst, :]
    cT = pT[2 * hp + nst : cin, :]
    xs2, b2, c2 = split(xs), split(bT), split(cT)
    tmp[...] = dot3(xs2, b2, NT) * eend
    own = pl.ds(pl.multiple_of(f * hpf, 8), hpf)
    st_out[:hpf, :] = tmp[own, :]
    last = e_ref[pl.ds(pl.multiple_of(f * hpf, 8), 8), tok - 128 : tok]
    st_out[hpf:, :] = jnp.broadcast_to(last[:, 127:128], (8, nst))
    for k in range(1, n):
        go(st_out, st_all.at[c], s_send.at[0, k], s_recv.at[0, c], (lax.rem(c + k, n), f))
    st_all[c] = st_out[...]

    upper = lax.broadcasted_iota(jnp.int32, (tok, tok), 0) <= lax.broadcasted_iota(
        jnp.int32, (tok, tok), 1)
    scores2 = split(jnp.where(upper, dot3(transposed(b2), c2, NN), 0.0))
    y_in = dot3(xs2, scores2, NN)
    sig = 1.0 / (1.0 + jnp.exp(-gate))
    silu = gate * sig

    for k in range(1, n):
        s = lax.rem(c + n - k, n)
        copy(st_out, st_all.at[s], s_send.at[0, k], s_recv.at[0, s], (s, f)).wait_recv()
    state = jnp.zeros((hpf, nst), f32)
    for k in range(n - 1):
        new = st_all[k, hpf : hpf + 1, :] * state + st_all[k, :hpf, :]
        state = jnp.where(k < c, new, state)
    s0_ref[own, :] = state
    for k in range(1, fs):
        go(s0_ref.at[own], s0_ref.at[own], s_send.at[1, k], s_recv.at[1, f], (c, lax.rem(f + k, fs)))
    for k in range(1, fs):
        p = lax.rem(f + fs - k, fs)
        rows = pl.ds(pl.multiple_of(p * hpf, 8), hpf)
        copy(s0_ref.at[rows], s0_ref.at[rows], s_send.at[1, k], s_recv.at[1, p], (c, p)).wait_recv()
    s02 = split(s0_ref[...])
    yT = (y_in + dot3(s02, c2, NN)) * e

    gain = gain_ref[...]
    gated = yT * silu
    r = lax.rsqrt(jnp.mean(gated * gated, axis=0, keepdims=True) + EPS)
    normed = (gated * r * gain).astype(bf16)
    u = pT[cin:, :] * gain
    dgated = r * u - gated * (r * r * r * jnp.mean(u * gated, axis=0, keepdims=True))
    dys2 = split(dgated * silu * e)
    tmp[...] = dot3(dys2, c2, NT)
    ad_out[...] = tmp[own, :].astype(bf16)
    for k in range(1, n):
        go(ad_out, ad_all.at[c], s_send.at[2, k], s_recv.at[2, c], (lax.rem(c + k, n), f))
    ad_all[c] = ad_out[...]
    gp[:hp, :] = (dgated * yT * (sig * (1.0 + gate * (1.0 - sig)))).astype(bf16)

    ro[...] = dot1(normed, gout_ref[...], NN)
    for q in range(outer):
        at = pl.ds(pl.multiple_of((q * 2 + 1 - y) * rows_out, 8), rows_out)
        ob1[q] = ro[at, :].astype(bf16)
    go(ob1, ob1r, o_send.at[0], o_recv.at[0], (yn, f))

    dscores2 = split(jnp.where(upper, dot3(transposed(xs2), dys2, NN), 0.0))
    gp[2 * hp + nst :, :] = (dot3(b2, dscores2, NN) + dot3(transposed(s02), dys2, NN)).astype(bf16)
    db = dot3(c2, dscores2, NT)
    dxs = dot3(dys2, scores2, NT)

    copy(ob1, ob1r, o_send.at[0], o_recv.at[0], (yn, f)).wait_recv()
    for q in range(outer):
        at = pl.ds(pl.multiple_of((q * 2 + y) * rows_out, 8), rows_out)
        total = ro[at, :] + ob1r[q].astype(f32)
        ro[at, :] = total
        ob2[q] = total.astype(bf16)

    for k in range(1, n):
        s = lax.rem(c + n - k, n)
        copy(ad_out, ad_all.at[s], s_send.at[2, k], s_recv.at[2, s], (s, f)).wait_recv()
    adj = jnp.zeros((hpf, nst), f32)
    for k in range(n - 1, 0, -1):
        new = st_all[k, hpf : hpf + 1, :] * adj + ad_all[k].astype(f32)
        adj = jnp.where(k > c, new, adj)
    g_ref[own, :] = adj
    for k in range(1, fs):
        go(g_ref.at[own], g_ref.at[own], s_send.at[3, k], s_recv.at[3, f], (c, lax.rem(f + k, fs)))
    for k in range(1, outer):
        q = lax.rem(z + k, outer)
        go(ob2.at[q], ob2r.at[z], o_send.at[k], o_recv.at[1 + z], (q * 2 + y, f))
    for k in range(1, fs):
        p = lax.rem(f + fs - k, fs)
        rows = pl.ds(pl.multiple_of(p * hpf, 8), hpf)
        copy(g_ref.at[rows], g_ref.at[rows], s_send.at[3, k], s_recv.at[3, p], (c, p)).wait_recv()
    g2 = split(g_ref[...] * eend)
    gp[hp : 2 * hp, :] = ((dxs + dot3(g2, b2, NN)) * einv).astype(bf16)
    gp[2 * hp : 2 * hp + nst, :] = (db + dot3(transposed(g2), xs2, NN)).astype(bf16)

    def rows_of(s):
        return pl.ds(pl.multiple_of(s * rows_in, 16), rows_in)

    far = order[::-1] + [0]
    for i, k in enumerate(far):
        q = lax.rem(z + k, outer)
        ib1[i] = dot1(gp[rows_of(q * 2 + 1 - y), :], hid_ref[...], NN).astype(bf16)
        go(ib1.at[i], ib1r.at[i], i_send.at[0, i], i_recv.at[0, i], (yn, f))
    for i, k in enumerate(far):
        q = lax.rem(z + k, outer)
        part = dot1(gp[rows_of(q * 2 + y), :], hid_ref[...], NN)
        copy(ib1.at[i], ib1r.at[i], i_send.at[0, i], i_recv.at[0, i], (yn, f)).wait_recv()
        part = part + ib1r[i].astype(f32)
        if k:
            ib2[i] = part.astype(bf16)
            go(ib2.at[i], ib2r.at[z], i_send.at[1, i], i_recv.at[1, z], (q * 2 + y, f))
        else:
            ri[...] = part

    acc = ro[pl.ds(pl.multiple_of(c * rows_out, 8), rows_out), :]
    for k in range(1, outer):
        q = lax.rem(z + k, outer)
        copy(ob2.at[q], ob2r.at[q], o_send.at[k], o_recv.at[1 + q], (q * 2 + y, f)).wait_recv()
        acc = acc + ob2r[q].astype(f32)
    acc = acc * (1.0 / root_tokens)
    ro[:rows_out, :] = acc
    nout_out[...] = jnp.broadcast_to(jnp.sum(acc * acc, axis=0, keepdims=True), (8, d))
    for k in range(1, n):
        go(nout_out, nout_all.at[c], n_send.at[0, k], n_recv.at[0, c], (lax.rem(c + k, n), f))
    nout_all[c] = nout_out[...]

    gpt = gp[...].T
    wi = wi_all[...].reshape(cin, d)
    gh_ref[...] = dot1(gpt, wi, NN).astype(bf16)

    weight = jnp.zeros((1, d), f32)
    for s in range(n):
        w = wo_all[s].astype(f32)
        weight = weight + jnp.sum(w * w, axis=0, keepdims=True)
    w = win_ref[...].astype(f32)
    weight_in = jnp.sum(w * w, axis=1, keepdims=True)

    acc = ri[...]
    for k in range(1, outer):
        q = lax.rem(z + k, outer)
        copy(ib2.at[0], ib2r.at[q], i_send.at[1, 0], i_recv.at[1, q], (q * 2 + y, f)).wait_recv()
        acc = acc + ib2r[q].astype(f32)
    acc = acc * (1.0 / root_tokens)
    ri[...] = acc
    at = lax.broadcasted_iota(jnp.int32, (rows_in, 128), 1)
    nin_out[...] = jnp.where(at < 64, jnp.sum(acc * acc, axis=1, keepdims=True), weight_in)
    for k in range(1, fs):
        go(nin_out, nin_all.at[f], n_send.at[1, k], n_recv.at[1, f], (c, lax.rem(f + k, fs)))
    nin_all[f] = nin_out[...]

    grad_square = nout_all[c, 0:1, :]
    for k in range(1, n):
        s = lax.rem(c + n - k, n)
        copy(nout_out, nout_all.at[s], n_send.at[0, k], n_recv.at[0, s], (s, f)).wait_recv()
        grad_square = grad_square + nout_all[s, 0:1, :]
    factor = jnp.minimum(1.0, clip_output * jnp.maximum(jnp.sqrt(weight), 0.001)
                         / jnp.maximum(jnp.sqrt(grad_square), 1e-06))
    gwo_ref[...] = ro[:rows_out, :] * factor

    square = nin_all[f]
    for k in range(1, fs):
        p = lax.rem(f + fs - k, fs)
        copy(nin_out, nin_all.at[p], n_send.at[1, k], n_recv.at[1, p], (c, p)).wait_recv()
        square = square + nin_all[p]
    root = jnp.sqrt(square)
    factor = jnp.minimum(1.0, clip_input * jnp.maximum(root[:, 64:65], 0.001)
                         / jnp.maximum(root[:, 0:1], 1e-06))
    gwi_ref[...] = ri[...] * factor
    for made in sent:
        made.wait_send()


def one_kernel(n, fs, hidden, w_in, decay, norm_gain, w_out, grad_out):
    tok, d = hidden.shape
    rows_in, rows_out = w_in.shape[0], w_out.shape[0]
    cin, hp = rows_in * n, rows_out * n
    nst = (cin - 2 * hp) // 2
    hpf, outer = hp // fs, n // 2
    half = (cin + hp) // 2
    size = half // PARTS
    V = pltpu.VMEM
    dma = pltpu.SemaphoreType.DMA
    scratch = [
        V((d, tok), bf16), V((d, tok), bf16), V((n, rows_in, d), bf16), V((n, rows_out, d), bf16),
        V((cin + hp, tok), f32), V((PARTS, size, tok), f32), V((PARTS, size, tok), bf16),
        V((PARTS, size, tok), bf16),
        V((hp, tok), f32), V((hpf + 8, nst), f32), V((n, hpf + 8, nst), f32), V((hp, nst), f32),
        V((hpf, nst), bf16), V((n, hpf, nst), bf16), V((hp, nst), f32),
        V((hp, d), f32), V((outer, rows_out, d), bf16), V((outer, rows_out, d), bf16),
        V((outer, rows_out, d), bf16), V((outer, rows_out, d), bf16),
        V((cin, tok), bf16), V((rows_in, d), f32),
        V((outer, rows_in, d), bf16), V((outer, rows_in, d), bf16),
        V((outer, rows_in, d), bf16), V((outer, rows_in, d), bf16),
        V((rows_in, 128), f32), V((fs, rows_in, 128), f32), V((8, d), f32), V((n, 8, d), f32),
        dma((2, n)), dma((2, n)), dma((3, PARTS)), dma((3, PARTS)), dma((4, n)), dma((4, n)),
        dma((1 + outer,)), dma((1 + outer,)), dma((2, outer)), dma((2, outer)),
        dma((2, n)), dma((2, n)), V((hp, nst), f32), V((PARTS, size, tok), f32),
    ]
    vm = pl.BlockSpec(memory_space=pltpu.VMEM)
    return pl.pallas_call(
        functools.partial(fused, n, fs, math.sqrt(tok * n), math.sqrt(d * fs)),
        out_shape=(
            jax.ShapeDtypeStruct((tok, d), bf16),
            jax.ShapeDtypeStruct((rows_in, d), f32),
            jax.ShapeDtypeStruct((rows_out, d), f32),
        ),
        in_specs=[vm] * 6,
        out_specs=(vm, vm, vm),
        scratch_shapes=scratch,
        compiler_params=pltpu.CompilerParams(
            collective_id=0, has_side_effects=True, vmem_limit_bytes=60 * 1024 * 1024),
    )(hidden, w_in, decay, norm_gain[:, None], w_out, grad_out)


def solution(mesh):
    n, fs = mesh.shape["ctx"], mesh.shape["fsdp"]

    def body(hidden, w_in, decay, norm_gain, w_out, grad_out):
        whole_tiles = w_in.shape[0] % 16 == 0 and w_out.shape[0] % 16 == 0
        if whole_tiles and fs == decay.shape[0] and fs % 2 == 0 and n % 2 == 0 and n >= 4:
            return one_kernel(n, fs, hidden, w_in, decay, norm_gain, w_out, grad_out)
        return local(hidden, w_in, decay, norm_gain, w_out, grad_out)

    return jax.shard_map(
        body,
        mesh=mesh,
        in_specs=(
            P("ctx", "fsdp"),
            P("ctx", "fsdp"),
            P(None, "ctx"),
            P(),
            P("ctx", "fsdp"),
            P("ctx", "fsdp"),
        ),
        out_specs=(P("ctx", "fsdp"), P("ctx", "fsdp"), P("ctx", "fsdp")),
        check_vma=False,
    )
```

```python
import functools
import math

import jax
import jax.numpy as jnp
from jax import lax
from jax.experimental import pallas as pl
from jax.experimental.pallas import tpu as pltpu
from jax.sharding import PartitionSpec as P

D = 4096
H = 4
P_SIZE = 64
N = 128
HP = 256


highest = lax.Precision.HIGHEST
clip_output = 10.0


def prefix(x, axis, combine, identity):
    count, index = (lax.axis_size(axis), lax.axis_index(axis))
    everything = jax.tree.map(lambda part: lax.all_gather(part, axis), x)
    start = jax.tree.map(
        lambda part, zero: jnp.broadcast_to(jnp.asarray(zero, part.dtype), part.shape), x, identity
    )

    def step(k, before):
        reached = k < index
        new = combine(before, jax.tree.map(lambda part: part[k], everything))
        return jax.tree.map(lambda a, b: jnp.where(reached, a, b), new, before)

    return lax.fori_loop(0, count, step, start)


def entering(x, axis, join, neutral):
    count = lax.axis_size(axis)
    place = lax.axis_index(axis)
    ahead = count - 1 - place
    gathered = jax.tree.map(
        lambda a, kind: lax.all_gather(a.astype(kind), axis),
        x,
        jax.tree.map(lambda a: jnp.bfloat16 if a.dtype == jnp.float32 else a.dtype, x),
    )
    state = jax.tree.map(lambda a, e: jnp.zeros_like(a) + jnp.asarray(e, a.dtype), x, neutral)

    def one(step, state):
        source = count - 1 - step
        return join(
            state,
            jax.tree.map(
                lambda a, own: lax.dynamic_index_in_dim(a, source, 0, False).astype(own.dtype),
                gathered,
                x,
            ),
        )

    return lax.fori_loop(0, ahead, one, state)


def split_columns(projection):
    return (
        projection[:, :HP],
        projection[:, HP : 2 * HP],
        projection[:, 2 * HP : 2 * HP + N],
        projection[:, 2 * HP + N :],
    )


def intra_block(x_part, b_part, c_part, log_decay):
    length = x_part.shape[0]
    cum_decay = jnp.cumsum(log_decay, axis=1)
    x_heads = x_part.reshape(length, H, P_SIZE)
    causal = jnp.arange(length)[:, None] >= jnp.arange(length)[None, :]
    gaps = jnp.where(causal[None], cum_decay[:, :, None] - cum_decay[:, None, :], 0.0)
    weights = jnp.where(causal[None], jnp.exp(gaps), 0.0)
    scores = jnp.dot(c_part, b_part.T, precision=highest)
    mixed = weights * scores[None]
    y_intra = jnp.einsum("hts,shp->thp", mixed, x_heads, precision=highest).reshape(
        length, H * P_SIZE
    )
    tail = jnp.exp(cum_decay[:, -1:] - cum_decay)
    weighted = x_heads * tail.T[:, :, None]
    state_part = jnp.einsum("shp,sn->hpn", weighted, b_part, precision=highest)
    return (y_intra, state_part, cum_decay)


def finish_block(gate_part, y_intra, c_part, start_state, cum_decay, norm_gain):
    length = c_part.shape[0]
    carried = jnp.einsum("hpn,tn->thp", start_state, c_part, precision=highest)
    carried = carried * jnp.exp(cum_decay).T[:, :, None]
    y_full = y_intra + carried.reshape(length, H * P_SIZE)
    gated = y_full * jax.nn.silu(gate_part)
    factor = lax.rsqrt(jnp.mean(gated * gated, axis=-1, keepdims=True) + 1e-05)
    return gated * factor * norm_gain


def carry_states(earlier, later):
    return (earlier[0] * later[0], later[0] * earlier[1] + later[1])


def carry_adjoint(earlier, later):
    return (earlier[0] * later[0], later[1] + later[0] * earlier[1])


def local(hidden, w_in, decay, norm_gain, w_out, grad_out):
    clip_input = math.sqrt(D)
    tok_rows = hidden.shape[0]
    root_tokens = math.sqrt(tok_rows * lax.axis_size("ctx"))
    contract_last = (((1,), (1,)), ((), ()))
    contract_first = (((0,), (0,)), ((), ()))
    partial_proj = lax.dot_general(
        hidden,
        lax.all_gather(w_in, "ctx", axis=0, tiled=True),
        contract_last,
        preferred_element_type=jnp.float32,
    )
    slab_out = lax.all_gather(w_out, "ctx", axis=0, tiled=True)
    partial_grad = lax.dot_general(
        grad_out, slab_out, contract_last, preferred_element_type=jnp.float32
    )
    projection, grad_normed = lax.psum((partial_proj, partial_grad), "fsdp")
    log_decay = jnp.log(decay)
    gate_part, x_part, b_part, c_part = split_columns(projection)

    def intra_only(x_value, b_value, c_value):
        return intra_block(x_value, b_value, c_value, log_decay)

    (y_intra, state_part, cum_decay), intra_pull = jax.vjp(intra_only, x_part, b_part, c_part)
    decay_total = jnp.exp(cum_decay[:, -1])[:, None, None]
    identity = (jnp.ones_like(decay_total), jnp.zeros_like(state_part))
    _, start_state = prefix((decay_total, state_part), "ctx", carry_states, identity)

    def finish_only(gate_value, intra_value, c_value, state_value):
        return finish_block(gate_value, intra_value, c_value, state_value, cum_decay, norm_gain)

    normed, finish_pull = jax.vjp(finish_only, gate_part, y_intra, c_part, start_state)
    grad_gate, grad_intra, grad_c_late, grad_start = finish_pull(grad_normed)
    _, grad_end = entering((decay_total, grad_start), "ctx", carry_adjoint, identity)
    grad_x, grad_b, grad_c_early = intra_pull((grad_intra, grad_end, jnp.zeros_like(cum_decay)))
    grad_projection = jnp.concatenate(
        [grad_gate, grad_x, grad_b, grad_c_early + grad_c_late], axis=1
    ).astype(jnp.bfloat16)
    columns = grad_projection
    grad_hidden = jnp.dot(
        columns, lax.all_gather(w_in, "ctx", axis=0, tiled=True), preferred_element_type=jnp.float32
    )
    columns = grad_projection
    raw_in = (
        lax.psum_scatter(
            lax.dot_general(columns, hidden, contract_first, preferred_element_type=jnp.float32),
            "ctx",
            scatter_dimension=0,
            tiled=True,
        )
        / root_tokens
    )
    weight_square = jnp.sum(jnp.square(w_in.astype(jnp.float32)), axis=1)
    weight_in, grad_in = lax.psum((weight_square, jnp.sum(raw_in * raw_in, axis=1)), "fsdp")
    factor_in = jnp.minimum(
        1.0,
        clip_input
        * jnp.maximum(jnp.sqrt(weight_in), 0.001)
        / jnp.maximum(jnp.sqrt(grad_in), 1e-06),
    )
    normed_rounded = normed.astype(jnp.bfloat16)
    weight_out = jnp.sqrt(jnp.sum(jnp.square(slab_out.astype(jnp.float32)), axis=0))
    raw_out = (
        lax.psum_scatter(
            lax.dot_general(
                normed_rounded, grad_out, contract_first, preferred_element_type=jnp.float32
            ),
            "ctx",
            scatter_dimension=0,
            tiled=True,
        )
        / root_tokens
    )
    grad_square = lax.psum(jnp.sum(raw_out * raw_out, axis=0), "ctx")
    factor_out = jnp.minimum(
        1.0,
        clip_output * jnp.maximum(weight_out, 0.001) / jnp.maximum(jnp.sqrt(grad_square), 1e-06),
    )
    return (
        grad_hidden.astype(jnp.bfloat16),
        raw_in * factor_in[:, None],
        raw_out * factor_out[None, :],
    )


NN = (((1,), (0,)), ((), ()))
NT = (((1,), (1,)), ((), ()))
TN = (((0,), (0,)), ((), ()))
MESH = pl.DeviceIdType.MESH
f32 = jnp.float32
bf16 = jnp.bfloat16
EPS = 1e-05


def split(a):
    hi = a.astype(bf16)
    return hi, (a - hi.astype(f32)).astype(bf16)


def dot1(a, b, dims):
    return lax.dot_general(a, b, dims, preferred_element_type=f32)


def dot3(a, b, dims):
    return dot1(a[0], b[0], dims) + (dot1(a[0], b[1], dims) + dot1(a[1], b[0], dims))


def transposed(pair):
    return pair[0].T, pair[1].T


def fused(
    n, fs, root_tokens, clip_input,
    hid_ref, win_ref, dec_ref, gain_ref, wout_ref, gout_ref,
    gh_ref, gwi_ref, gwo_ref,
    hidT, goutT, wi_all, wo_all, pT, buf, core_in, x_out, x_in, c_in, e_out, e_all,
    e_ref, st_out, st_all, s0_ref, ad_out, ad_all, g_ref,
    ro, ob1, ob1r, ob2, ob2r, gp, ri, ib1, ib1r, ib2, ib2r,
    nin_out, nin_all, nout_out, nout_all,
    g_send, g_recv, p_send, p_recv, s_send, s_recv, o_send, o_recv, i_send, i_recv,
    n_send, n_recv, tmp,
):
    c = lax.axis_index("ctx")
    f = lax.axis_index("fsdp")
    outer = n // 2
    z, y = c // 2, lax.rem(c, 2)
    yn = c + 1 - 2 * y
    core = lax.rem(f, 2)
    fcore = f + 1 - 2 * core
    fx = lax.rem(f + fs // 2, fs)
    rows_in, d = win_ref.shape
    rows_out = wout_ref.shape[0]
    tok = hid_ref.shape[0]
    cin, hp = rows_in * n, rows_out * n
    nst = (cin - 2 * hp) // 2
    hpf = hp // fs

    def copy(src, dst, ssem, rsem, dev):
        return pltpu.make_async_remote_copy(
            src_ref=src, dst_ref=dst, send_sem=ssem, recv_sem=rsem,
            device_id=dev, device_id_type=MESH)

    sent = []

    def go(*args, when=None):
        if when is None:
            copy(*args).start()
        else:
            pl.when(when)(lambda: copy(*args).start())
        sent.append((when, args))

    def arrive(*args, when=None):
        if when is None:
            copy(*args).wait_recv()
        else:
            pl.when(when)(lambda: copy(*args).wait_recv())

    barrier = pltpu.get_barrier_semaphore()
    for k in range(1, n):
        pl.semaphore_signal(barrier, inc=1, device_id=(lax.rem(c + k, n), f), device_id_type=MESH)
    for k in range(1, fs):
        pl.semaphore_signal(barrier, inc=1, device_id=(c, lax.rem(f + k, fs)), device_id_type=MESH)
    pl.semaphore_wait(barrier, n + fs - 2)

    both = ((win_ref, wi_all), (wout_ref, wo_all))
    up = jnp.minimum(z + 1, outer - 1) * 2 + y
    down = jnp.maximum(z - 1, 0) * 2 + y
    order = [1, outer - 1] + list(range(2, outer - 1))
    for a, (src, dst) in enumerate(both):
        go(src, dst.at[c], g_send.at[0, a, c], g_recv.at[a, c], (up, f), when=z < outer - 1)
        go(src, dst.at[c], g_send.at[1, a, c], g_recv.at[a, c], (down, f), when=z > 0)
        go(src, dst.at[c], g_send.at[2, a, c], g_recv.at[a, c], (yn, f))
    wi_all[c] = win_ref[...]
    wo_all[c] = wout_ref[...]
    hidT[...] = hid_ref[...].T
    goutT[...] = gout_ref[...].T

    decay = dec_ref[...]
    lane = lax.broadcasted_iota(jnp.int32, decay.shape, 1)
    shift = 1
    while shift < tok:
        decay = decay * jnp.where(lane >= shift, pltpu.roll(decay, shift, 1), 1.0)
        shift *= 2
    heads = decay.shape[0]
    for h in range(heads):
        e_ref[h * (hp // heads) : (h + 1) * (hp // heads), :] = jnp.broadcast_to(
            decay[h : h + 1], (hp // heads, tok))

    e_out[...] = jnp.broadcast_to(
        e_ref[pl.ds(pl.multiple_of(f * hpf, 8), 8), tok - 128 : tok][:, 127:128], (8, nst))
    e_all[c] = e_out[...]
    for k in range(1, n):
        go(e_out, e_all.at[c], s_send.at[4, k], s_recv.at[4, c], (lax.rem(c + k, n), f))

    hi, ho = rows_in // 2, rows_out // 2
    half = hi + ho
    mine = pl.ds(pl.multiple_of(core * half, 8), half)
    other = pl.ds(pl.multiple_of((1 - core) * half, 8), half)

    def place(s, which, value):
        pT[pl.ds(pl.multiple_of(s * rows_in + which * hi, 8), hi), :] = value[:hi]
        pT[pl.ds(pl.multiple_of(cin + s * rows_out + which * ho, 8), ho), :] = value[hi:]

    def to_pair(s):
        return (buf.at[s, other], core_in.at[s], p_send.at[0, s], p_recv.at[0, s], (c, fcore))

    def across(s):
        return (x_out.at[s], x_in.at[s], p_send.at[1, s], p_recv.at[1, s], (c, fx))

    def back(s):
        return (buf.at[s, mine], c_in.at[s], p_send.at[2, s], p_recv.at[2, s], (c, fcore))

    def project(s):
        left = dot1(wi_all[s], hidT[...], NN)
        right = dot1(wo_all[s], goutT[...], NN)
        buf[s, :hi] = left[:hi]
        buf[s, hi:half] = right[:ho]
        buf[s, half : half + hi] = left[hi:]
        buf[s, half + hi :] = right[ho:]
        copy(*to_pair(s)).start()

    def pair_sum(s):
        copy(*to_pair(s)).wait_recv()
        total = buf[s, mine] + core_in[s]
        buf[s, mine] = total
        x_out[s] = total.astype(bf16)
        copy(*across(s)).start()

    def full_sum(s):
        copy(*across(s)).wait_recv()
        total = buf[s, mine] + x_in[s].astype(f32)
        buf[s, mine] = total
        copy(*back(s)).start()
        place(s, core, total)

    def collect(s):
        copy(*back(s)).wait_recv()
        place(s, 1 - core, c_in[s])

    def landed(s, fwd, across_pair):
        for a, (src, dst) in enumerate(both):
            copy(dst.at[s], dst.at[s], g_send.at[2, a, s], g_recv.at[a, s], (yn, f)).wait_recv()
            if fwd is not None:
                has, to, way = fwd
                pl.when(has)(lambda: copy(
                    dst.at[s], dst.at[s], g_send.at[way, a, s], g_recv.at[a, s], (to, f)).start())
            if across_pair:
                copy(dst.at[s], dst.at[s], g_send.at[2, a, s], g_recv.at[a, s], (yn, f)).start()

    def row(k, way):
        there = z - k if way == 0 else z + k
        has = there >= 0 if way == 0 else there < outer
        q = jnp.maximum(there, 0) if way == 0 else jnp.minimum(there, outer - 1)
        fwd = (z < outer - 1, up, 0) if way == 0 else (z > 0, down, 1)
        return has, q, fwd

    events = [(None, c, None, False, False)]
    later = [(None, z * 2 + 1 - y, None, True, False)]
    for k in range(1, outer):
        for way in (0, 1):
            has, q, fwd = row(k, way)
            events.append((has, q * 2 + y, fwd, True, True))
        events.extend(later)
        later = []
        for way in (0, 1):
            has, q, fwd = row(k, way)
            later.append((has, q * 2 + 1 - y, None, True, False))
    events.extend(later)

    def under(has, fn, *args):
        if has is None:
            fn(*args)
        else:
            pl.when(has)(lambda: fn(*args))

    def take(s, fwd, wait, across_pair):
        if wait:
            landed(s, fwd, across_pair)
        project(s)

    def release(s, fwd, across_pair):
        for args in (to_pair(s), across(s), back(s)):
            copy(*args).wait_send()
        for a, (src, dst) in enumerate(both):
            def there(way, to):
                copy(dst.at[s], dst.at[s], g_send.at[way, a, s], g_recv.at[a, s],
                     (to, f)).wait_send()
            if fwd is not None:
                under(fwd[0], there, fwd[2], fwd[1])
            if across_pair:
                there(2, yn)

    total_events = len(events)
    for i in range(total_events + 5):
        if i < total_events:
            has, s, fwd, wait, across_pair = events[i]
            under(has, take, s, fwd, wait, across_pair)
        for lag, fn in ((1, pair_sum), (3, full_sum), (5, collect)):
            if 0 <= i - lag < total_events:
                under(events[i - lag][0], fn, events[i - lag][1])

    e = e_ref[...]
    einv = 1.0 / e
    eend = e[:, tok - 1 : tok]
    gate = pT[:hp, :]
    xs = pT[hp : 2 * hp, :] * einv
    bT = pT[2 * hp : 2 * hp + nst, :]
    cT = pT[2 * hp + nst : cin, :]
    xs2, b2, c2 = split(xs), split(bT), split(cT)
    tmp[...] = dot3(xs2, b2, NT) * eend
    own = pl.ds(pl.multiple_of(f * hpf, 8), hpf)
    st_out[...] = tmp[own, :]
    for k in range(n - 1, 0, -1):
        go(st_out, st_all.at[c], s_send.at[0, k], s_recv.at[0, c],
           (jnp.minimum(c + k, n - 1), f), when=c + k < n)

    upper = lax.broadcasted_iota(jnp.int32, (tok, tok), 0) <= lax.broadcasted_iota(
        jnp.int32, (tok, tok), 1)
    scores2 = split(jnp.where(upper, dot3(transposed(b2), c2, NN), 0.0))
    y_in = dot3(xs2, scores2, NN)
    sig = 1.0 / (1.0 + jnp.exp(-gate))
    silu = gate * sig

    for k in range(1, n):
        s = lax.rem(c + n - k, n)
        arrive(e_out, e_all.at[s], s_send.at[4, k], s_recv.at[4, s], (s, f))
        s = jnp.maximum(c - k, 0)
        arrive(st_out, st_all.at[s], s_send.at[0, k], s_recv.at[0, s], (s, f), when=c - k >= 0)
    state = jnp.zeros((hpf, nst), f32)
    for k in range(n - 1):
        new = e_all[k, 0:1, :] * state + st_all[k]
        state = jnp.where(k < c, new, state)
    s0_ref[own, :] = state
    for k in range(1, fs):
        go(s0_ref.at[own], s0_ref.at[own], s_send.at[1, k], s_recv.at[1, f], (c, lax.rem(f + k, fs)))
    for k in range(1, fs):
        p = lax.rem(f + fs - k, fs)
        rows = pl.ds(pl.multiple_of(p * hpf, 8), hpf)
        copy(s0_ref.at[rows], s0_ref.at[rows], s_send.at[1, k], s_recv.at[1, p], (c, p)).wait_recv()
    s02 = split(s0_ref[...])
    yT = (y_in + dot3(s02, c2, NN)) * e

    gain = gain_ref[...]
    gated = yT * silu
    r = lax.rsqrt(jnp.mean(gated * gated, axis=0, keepdims=True) + EPS)
    normed = (gated * r * gain).astype(bf16)
    u = pT[cin:, :] * gain
    dgated = r * u - gated * (r * r * r * jnp.mean(u * gated, axis=0, keepdims=True))
    dys2 = split(dgated * silu * e)
    tmp[...] = dot3(dys2, c2, NT)
    ad_out[...] = tmp[own, :].astype(bf16)
    for k in range(n - 1, 0, -1):
        go(ad_out, ad_all.at[c], s_send.at[2, k], s_recv.at[2, c],
           (jnp.maximum(c - k, 0), f), when=c - k >= 0)
    gp[:hp, :] = (dgated * yT * (sig * (1.0 + gate * (1.0 - sig)))).astype(bf16)

    ro[...] = dot1(normed, gout_ref[...], NN)
    for q in range(outer):
        at = pl.ds(pl.multiple_of((q * 2 + 1 - y) * rows_out, 8), rows_out)
        ob1[q] = ro[at, :].astype(bf16)
    go(ob1, ob1r, o_send.at[0], o_recv.at[0], (yn, f))

    dscores2 = split(jnp.where(upper, dot3(transposed(xs2), dys2, NN), 0.0))
    gp[2 * hp + nst :, :] = (dot3(b2, dscores2, NN) + dot3(transposed(s02), dys2, NN)).astype(bf16)
    db = dot3(c2, dscores2, NT)
    dxs = dot3(dys2, scores2, NT)

    copy(ob1, ob1r, o_send.at[0], o_recv.at[0], (yn, f)).wait_recv()
    for q in range(outer):
        at = pl.ds(pl.multiple_of((q * 2 + y) * rows_out, 8), rows_out)
        total = ro[at, :] + ob1r[q].astype(f32)
        ro[at, :] = total
        ob2[q] = total.astype(bf16)

    for k in range(1, n):
        s = jnp.minimum(c + k, n - 1)
        arrive(ad_out, ad_all.at[s], s_send.at[2, k], s_recv.at[2, s], (s, f), when=c + k < n)
    adj = jnp.zeros((hpf, nst), f32)
    for k in range(n - 1, 0, -1):
        new = e_all[k, 0:1, :] * adj + ad_all[k].astype(f32)
        adj = jnp.where(k > c, new, adj)
    g_ref[own, :] = adj
    for k in range(1, fs):
        go(g_ref.at[own], g_ref.at[own], s_send.at[3, k], s_recv.at[3, f], (c, lax.rem(f + k, fs)))
    for k in range(1, outer):
        q = lax.rem(z + k, outer)
        go(ob2.at[q], ob2r.at[z], o_send.at[k], o_recv.at[1 + z], (q * 2 + y, f))
    for k in range(1, fs):
        p = lax.rem(f + fs - k, fs)
        rows = pl.ds(pl.multiple_of(p * hpf, 8), hpf)
        copy(g_ref.at[rows], g_ref.at[rows], s_send.at[3, k], s_recv.at[3, p], (c, p)).wait_recv()
    g2 = split(g_ref[...] * eend)
    gp[hp : 2 * hp, :] = ((dxs + dot3(g2, b2, NN)) * einv).astype(bf16)
    gp[2 * hp : 2 * hp + nst, :] = (db + dot3(transposed(g2), xs2, NN)).astype(bf16)

    def rows_of(s):
        return pl.ds(pl.multiple_of(s * rows_in, 16), rows_in)

    far = order[::-1] + [0]
    for i, k in enumerate(far):
        q = lax.rem(z + k, outer)
        ib1[i] = dot1(gp[rows_of(q * 2 + 1 - y), :], hid_ref[...], NN).astype(bf16)
        go(ib1.at[i], ib1r.at[i], i_send.at[0, i], i_recv.at[0, i], (yn, f))
    for i, k in enumerate(far):
        q = lax.rem(z + k, outer)
        part = dot1(gp[rows_of(q * 2 + y), :], hid_ref[...], NN)
        copy(ib1.at[i], ib1r.at[i], i_send.at[0, i], i_recv.at[0, i], (yn, f)).wait_recv()
        part = part + ib1r[i].astype(f32)
        if k:
            ib2[i] = part.astype(bf16)
            go(ib2.at[i], ib2r.at[z], i_send.at[1, i], i_recv.at[1, z], (q * 2 + y, f))
        else:
            ri[...] = part

    acc = ro[pl.ds(pl.multiple_of(c * rows_out, 8), rows_out), :]
    for k in range(1, outer):
        q = lax.rem(z + k, outer)
        copy(ob2.at[q], ob2r.at[q], o_send.at[k], o_recv.at[1 + q], (q * 2 + y, f)).wait_recv()
        acc = acc + ob2r[q].astype(f32)
    acc = acc * (1.0 / root_tokens)
    ro[:rows_out, :] = acc
    nout_out[...] = jnp.broadcast_to(jnp.sum(acc * acc, axis=0, keepdims=True), (8, d))
    for k in range(1, n):
        go(nout_out, nout_all.at[c], n_send.at[0, k], n_recv.at[0, c], (lax.rem(c + k, n), f))
    nout_all[c] = nout_out[...]

    gpt = gp[...].T
    wi = wi_all[...].reshape(cin, d)
    gh_ref[...] = dot1(gpt, wi, NN).astype(bf16)

    weight = jnp.zeros((1, d), f32)
    for s in range(n):
        w = wo_all[s].astype(f32)
        weight = weight + jnp.sum(w * w, axis=0, keepdims=True)
    w = win_ref[...].astype(f32)
    weight_in = jnp.sum(w * w, axis=1, keepdims=True)

    acc = ri[...]
    for k in range(1, outer):
        q = lax.rem(z + k, outer)
        copy(ib2.at[0], ib2r.at[q], i_send.at[1, 0], i_recv.at[1, q], (q * 2 + y, f)).wait_recv()
        acc = acc + ib2r[q].astype(f32)
    acc = acc * (1.0 / root_tokens)
    ri[...] = acc
    at = lax.broadcasted_iota(jnp.int32, (rows_in, 128), 1)
    nin_out[...] = jnp.where(at < 64, jnp.sum(acc * acc, axis=1, keepdims=True), weight_in)
    for k in range(1, fs):
        go(nin_out, nin_all.at[f], n_send.at[1, k], n_recv.at[1, f], (c, lax.rem(f + k, fs)))
    nin_all[f] = nin_out[...]

    grad_square = nout_all[c, 0:1, :]
    for k in range(1, n):
        s = lax.rem(c + n - k, n)
        copy(nout_out, nout_all.at[s], n_send.at[0, k], n_recv.at[0, s], (s, f)).wait_recv()
        grad_square = grad_square + nout_all[s, 0:1, :]
    factor = jnp.minimum(1.0, clip_output * jnp.maximum(jnp.sqrt(weight), 0.001)
                         / jnp.maximum(jnp.sqrt(grad_square), 1e-06))
    gwo_ref[...] = ro[:rows_out, :] * factor

    square = nin_all[f]
    for k in range(1, fs):
        p = lax.rem(f + fs - k, fs)
        copy(nin_out, nin_all.at[p], n_send.at[1, k], n_recv.at[1, p], (c, p)).wait_recv()
        square = square + nin_all[p]
    root = jnp.sqrt(square)
    factor = jnp.minimum(1.0, clip_input * jnp.maximum(root[:, 64:65], 0.001)
                         / jnp.maximum(root[:, 0:1], 1e-06))
    gwi_ref[...] = ri[...] * factor
    for has, args in sent:
        under(has, lambda args: copy(*args).wait_send(), args)
    for has, s, fwd, wait, across_pair in events:
        under(has, release, s, fwd, across_pair)


def one_kernel(n, fs, hidden, w_in, decay, norm_gain, w_out, grad_out):
    tok, d = hidden.shape
    rows_in, rows_out = w_in.shape[0], w_out.shape[0]
    cin, hp = rows_in * n, rows_out * n
    nst = (cin - 2 * hp) // 2
    hpf, outer = hp // fs, n // 2
    half = (rows_in + rows_out) // 2
    V = pltpu.VMEM
    dma = pltpu.SemaphoreType.DMA
    scratch = [
        V((d, tok), bf16), V((d, tok), bf16), V((n, rows_in, d), bf16), V((n, rows_out, d), bf16),
        V((cin + hp, tok), f32), V((n, 2 * half, tok), f32), V((n, half, tok), f32),
        V((n, half, tok), bf16), V((n, half, tok), bf16), V((n, half, tok), f32),
        V((8, nst), f32), V((n, 8, nst), f32),
        V((hp, tok), f32), V((hpf, nst), f32), V((n, hpf, nst), f32), V((hp, nst), f32),
        V((hpf, nst), bf16), V((n, hpf, nst), bf16), V((hp, nst), f32),
        V((hp, d), f32), V((outer, rows_out, d), bf16), V((outer, rows_out, d), bf16),
        V((outer, rows_out, d), bf16), V((outer, rows_out, d), bf16),
        V((cin, tok), bf16), V((rows_in, d), f32),
        V((outer, rows_in, d), bf16), V((outer, rows_in, d), bf16),
        V((outer, rows_in, d), bf16), V((outer, rows_in, d), bf16),
        V((rows_in, 128), f32), V((fs, rows_in, 128), f32), V((8, d), f32), V((n, 8, d), f32),
        dma((3, 2, n)), dma((2, n)), dma((3, n)), dma((3, n)), dma((5, n)), dma((5, n)),
        dma((1 + outer,)), dma((1 + outer,)), dma((2, outer)), dma((2, outer)),
        dma((2, n)), dma((2, n)), V((hp, nst), f32),
    ]
    vm = pl.BlockSpec(memory_space=pltpu.VMEM)
    return pl.pallas_call(
        functools.partial(fused, n, fs, math.sqrt(tok * n), math.sqrt(d * fs)),
        out_shape=(
            jax.ShapeDtypeStruct((tok, d), bf16),
            jax.ShapeDtypeStruct((rows_in, d), f32),
            jax.ShapeDtypeStruct((rows_out, d), f32),
        ),
        in_specs=[vm] * 6,
        out_specs=(vm, vm, vm),
        scratch_shapes=scratch,
        compiler_params=pltpu.CompilerParams(
            collective_id=0, has_side_effects=True, vmem_limit_bytes=60 * 1024 * 1024),
    )(hidden, w_in, decay, norm_gain[:, None], w_out, grad_out)


def solution(mesh):
    n, fs = mesh.shape["ctx"], mesh.shape["fsdp"]

    def body(hidden, w_in, decay, norm_gain, w_out, grad_out):
        whole_tiles = w_in.shape[0] % 16 == 0 and w_out.shape[0] % 16 == 0
        if whole_tiles and fs == decay.shape[0] and fs % 2 == 0 and n % 2 == 0 and n >= 4:
            return one_kernel(n, fs, hidden, w_in, decay, norm_gain, w_out, grad_out)
        return local(hidden, w_in, decay, norm_gain, w_out, grad_out)

    return jax.shard_map(
        body,
        mesh=mesh,
        in_specs=(
            P("ctx", "fsdp"),
            P("ctx", "fsdp"),
            P(None, "ctx"),
            P(),
            P("ctx", "fsdp"),
            P("ctx", "fsdp"),
        ),
        out_specs=(P("ctx", "fsdp"), P("ctx", "fsdp"), P("ctx", "fsdp")),
        check_vma=False,
    )
```

```python
import functools
import math

import jax
import jax.numpy as jnp
from jax import lax
from jax.experimental import pallas as pl
from jax.experimental.pallas import tpu as pltpu
from jax.sharding import PartitionSpec as P

D = 4096
H = 4
P_SIZE = 64
N = 128
HP = 256


highest = lax.Precision.HIGHEST
clip_output = 10.0


def prefix(x, axis, combine, identity):
    count, index = (lax.axis_size(axis), lax.axis_index(axis))
    everything = jax.tree.map(lambda part: lax.all_gather(part, axis), x)
    start = jax.tree.map(
        lambda part, zero: jnp.broadcast_to(jnp.asarray(zero, part.dtype), part.shape), x, identity
    )

    def step(k, before):
        reached = k < index
        new = combine(before, jax.tree.map(lambda part: part[k], everything))
        return jax.tree.map(lambda a, b: jnp.where(reached, a, b), new, before)

    return lax.fori_loop(0, count, step, start)


def entering(x, axis, join, neutral):
    count = lax.axis_size(axis)
    place = lax.axis_index(axis)
    ahead = count - 1 - place
    gathered = jax.tree.map(
        lambda a, kind: lax.all_gather(a.astype(kind), axis),
        x,
        jax.tree.map(lambda a: jnp.bfloat16 if a.dtype == jnp.float32 else a.dtype, x),
    )
    state = jax.tree.map(lambda a, e: jnp.zeros_like(a) + jnp.asarray(e, a.dtype), x, neutral)

    def one(step, state):
        source = count - 1 - step
        return join(
            state,
            jax.tree.map(
                lambda a, own: lax.dynamic_index_in_dim(a, source, 0, False).astype(own.dtype),
                gathered,
                x,
            ),
        )

    return lax.fori_loop(0, ahead, one, state)


def split_columns(projection):
    return (
        projection[:, :HP],
        projection[:, HP : 2 * HP],
        projection[:, 2 * HP : 2 * HP + N],
        projection[:, 2 * HP + N :],
    )


def intra_block(x_part, b_part, c_part, log_decay):
    length = x_part.shape[0]
    cum_decay = jnp.cumsum(log_decay, axis=1)
    x_heads = x_part.reshape(length, H, P_SIZE)
    causal = jnp.arange(length)[:, None] >= jnp.arange(length)[None, :]
    gaps = jnp.where(causal[None], cum_decay[:, :, None] - cum_decay[:, None, :], 0.0)
    weights = jnp.where(causal[None], jnp.exp(gaps), 0.0)
    scores = jnp.dot(c_part, b_part.T, precision=highest)
    mixed = weights * scores[None]
    y_intra = jnp.einsum("hts,shp->thp", mixed, x_heads, precision=highest).reshape(
        length, H * P_SIZE
    )
    tail = jnp.exp(cum_decay[:, -1:] - cum_decay)
    weighted = x_heads * tail.T[:, :, None]
    state_part = jnp.einsum("shp,sn->hpn", weighted, b_part, precision=highest)
    return (y_intra, state_part, cum_decay)


def finish_block(gate_part, y_intra, c_part, start_state, cum_decay, norm_gain):
    length = c_part.shape[0]
    carried = jnp.einsum("hpn,tn->thp", start_state, c_part, precision=highest)
    carried = carried * jnp.exp(cum_decay).T[:, :, None]
    y_full = y_intra + carried.reshape(length, H * P_SIZE)
    gated = y_full * jax.nn.silu(gate_part)
    factor = lax.rsqrt(jnp.mean(gated * gated, axis=-1, keepdims=True) + 1e-05)
    return gated * factor * norm_gain


def carry_states(earlier, later):
    return (earlier[0] * later[0], later[0] * earlier[1] + later[1])


def carry_adjoint(earlier, later):
    return (earlier[0] * later[0], later[1] + later[0] * earlier[1])


def local(hidden, w_in, decay, norm_gain, w_out, grad_out):
    clip_input = math.sqrt(D)
    tok_rows = hidden.shape[0]
    root_tokens = math.sqrt(tok_rows * lax.axis_size("ctx"))
    contract_last = (((1,), (1,)), ((), ()))
    contract_first = (((0,), (0,)), ((), ()))
    partial_proj = lax.dot_general(
        hidden,
        lax.all_gather(w_in, "ctx", axis=0, tiled=True),
        contract_last,
        preferred_element_type=jnp.float32,
    )
    slab_out = lax.all_gather(w_out, "ctx", axis=0, tiled=True)
    partial_grad = lax.dot_general(
        grad_out, slab_out, contract_last, preferred_element_type=jnp.float32
    )
    projection, grad_normed = lax.psum((partial_proj, partial_grad), "fsdp")
    log_decay = jnp.log(decay)
    gate_part, x_part, b_part, c_part = split_columns(projection)

    def intra_only(x_value, b_value, c_value):
        return intra_block(x_value, b_value, c_value, log_decay)

    (y_intra, state_part, cum_decay), intra_pull = jax.vjp(intra_only, x_part, b_part, c_part)
    decay_total = jnp.exp(cum_decay[:, -1])[:, None, None]
    identity = (jnp.ones_like(decay_total), jnp.zeros_like(state_part))
    _, start_state = prefix((decay_total, state_part), "ctx", carry_states, identity)

    def finish_only(gate_value, intra_value, c_value, state_value):
        return finish_block(gate_value, intra_value, c_value, state_value, cum_decay, norm_gain)

    normed, finish_pull = jax.vjp(finish_only, gate_part, y_intra, c_part, start_state)
    grad_gate, grad_intra, grad_c_late, grad_start = finish_pull(grad_normed)
    _, grad_end = entering((decay_total, grad_start), "ctx", carry_adjoint, identity)
    grad_x, grad_b, grad_c_early = intra_pull((grad_intra, grad_end, jnp.zeros_like(cum_decay)))
    grad_projection = jnp.concatenate(
        [grad_gate, grad_x, grad_b, grad_c_early + grad_c_late], axis=1
    ).astype(jnp.bfloat16)
    columns = grad_projection
    grad_hidden = jnp.dot(
        columns, lax.all_gather(w_in, "ctx", axis=0, tiled=True), preferred_element_type=jnp.float32
    )
    columns = grad_projection
    raw_in = (
        lax.psum_scatter(
            lax.dot_general(columns, hidden, contract_first, preferred_element_type=jnp.float32),
            "ctx",
            scatter_dimension=0,
            tiled=True,
        )
        / root_tokens
    )
    weight_square = jnp.sum(jnp.square(w_in.astype(jnp.float32)), axis=1)
    weight_in, grad_in = lax.psum((weight_square, jnp.sum(raw_in * raw_in, axis=1)), "fsdp")
    factor_in = jnp.minimum(
        1.0,
        clip_input
        * jnp.maximum(jnp.sqrt(weight_in), 0.001)
        / jnp.maximum(jnp.sqrt(grad_in), 1e-06),
    )
    normed_rounded = normed.astype(jnp.bfloat16)
    weight_out = jnp.sqrt(jnp.sum(jnp.square(slab_out.astype(jnp.float32)), axis=0))
    raw_out = (
        lax.psum_scatter(
            lax.dot_general(
                normed_rounded, grad_out, contract_first, preferred_element_type=jnp.float32
            ),
            "ctx",
            scatter_dimension=0,
            tiled=True,
        )
        / root_tokens
    )
    grad_square = lax.psum(jnp.sum(raw_out * raw_out, axis=0), "ctx")
    factor_out = jnp.minimum(
        1.0,
        clip_output * jnp.maximum(weight_out, 0.001) / jnp.maximum(jnp.sqrt(grad_square), 1e-06),
    )
    return (
        grad_hidden.astype(jnp.bfloat16),
        raw_in * factor_in[:, None],
        raw_out * factor_out[None, :],
    )


NN = (((1,), (0,)), ((), ()))
NT = (((1,), (1,)), ((), ()))
TN = (((0,), (0,)), ((), ()))
MESH = pl.DeviceIdType.MESH
f32 = jnp.float32
bf16 = jnp.bfloat16
EPS = 1e-05


def split(a):
    hi = a.astype(bf16)
    return hi, (a - hi.astype(f32)).astype(bf16)


def dot1(a, b, dims):
    return lax.dot_general(a, b, dims, preferred_element_type=f32)


def dot3(a, b, dims):
    return dot1(a[0], b[0], dims) + (dot1(a[0], b[1], dims) + dot1(a[1], b[0], dims))


def transposed(pair):
    return pair[0].T, pair[1].T


def fused(
    n, fs, root_tokens, clip_input,
    hid_ref, win_ref, dec_ref, gain_ref, wout_ref, gout_ref,
    gh_ref, gwi_ref, gwo_ref,
    hidT, goutT, wi_all, wo_all, pT, buf, core_in, x_out, x_in, c_in, e_out, e_all,
    e_ref, st_out, st_all, s0_ref, ad_out, ad_all, g_ref,
    ro, ob1, ob1r, ob2, ob2r, gp, ri, ib1, ib1r, ib2, ib2r,
    nin_out, nin_all, nout_out, nout_all,
    g_send, g_recv, p_send, p_recv, s_send, s_recv, o_send, o_recv, i_send, i_recv,
    n_send, n_recv, tmp,
):
    c = lax.axis_index("ctx")
    f = lax.axis_index("fsdp")
    outer = n // 2
    z, y = c // 2, lax.rem(c, 2)
    yn = c + 1 - 2 * y
    core = lax.rem(f, 2)
    fcore = f + 1 - 2 * core
    fx = lax.rem(f + fs // 2, fs)
    rows_in, d = win_ref.shape
    rows_out = wout_ref.shape[0]
    tok = hid_ref.shape[0]
    cin, hp = rows_in * n, rows_out * n
    nst = (cin - 2 * hp) // 2
    hpf = hp // fs

    def copy(src, dst, ssem, rsem, dev):
        return pltpu.make_async_remote_copy(
            src_ref=src, dst_ref=dst, send_sem=ssem, recv_sem=rsem,
            device_id=dev, device_id_type=MESH)

    sent = []

    def go(*args, when=None):
        if when is None:
            copy(*args).start()
        else:
            pl.when(when)(lambda: copy(*args).start())
        sent.append((when, args))

    def arrive(*args, when=None):
        if when is None:
            copy(*args).wait_recv()
        else:
            pl.when(when)(lambda: copy(*args).wait_recv())

    barrier = pltpu.get_barrier_semaphore()
    for k in range(1, n):
        pl.semaphore_signal(barrier, inc=1, device_id=(lax.rem(c + k, n), f), device_id_type=MESH)
    for k in range(1, fs):
        pl.semaphore_signal(barrier, inc=1, device_id=(c, lax.rem(f + k, fs)), device_id_type=MESH)
    pl.semaphore_wait(barrier, n + fs - 2)

    both = ((win_ref, wi_all), (wout_ref, wo_all))
    up = jnp.minimum(z + 1, outer - 1) * 2 + y
    down = jnp.maximum(z - 1, 0) * 2 + y
    order = [1, outer - 1] + list(range(2, outer - 1))
    for a, (src, dst) in enumerate(both):
        go(src, dst.at[c], g_send.at[0, a, c], g_recv.at[a, c], (up, f), when=z < outer - 1)
        go(src, dst.at[c], g_send.at[1, a, c], g_recv.at[a, c], (down, f), when=z > 0)
        go(src, dst.at[c], g_send.at[2, a, c], g_recv.at[a, c], (yn, f))
    wi_all[c] = win_ref[...]
    wo_all[c] = wout_ref[...]
    hidT[...] = hid_ref[...].T
    goutT[...] = gout_ref[...].T

    decay = dec_ref[...]
    lane = lax.broadcasted_iota(jnp.int32, decay.shape, 1)
    shift = 1
    while shift < tok:
        decay = decay * jnp.where(lane >= shift, pltpu.roll(decay, shift, 1), 1.0)
        shift *= 2
    heads = decay.shape[0]
    for h in range(heads):
        e_ref[h * (hp // heads) : (h + 1) * (hp // heads), :] = jnp.broadcast_to(
            decay[h : h + 1], (hp // heads, tok))

    e_out[...] = jnp.broadcast_to(
        e_ref[pl.ds(pl.multiple_of(f * hpf, 8), 8), tok - 128 : tok][:, 127:128], (8, nst))
    e_all[c] = e_out[...]
    for k in range(1, n):
        go(e_out, e_all.at[c], s_send.at[4, k], s_recv.at[4, c], (lax.rem(c + k, n), f))

    hi, ho = rows_in // 2, rows_out // 2
    half = hi + ho
    mine = pl.ds(pl.multiple_of(core * half, 8), half)
    other = pl.ds(pl.multiple_of((1 - core) * half, 8), half)

    def place(s, which, value):
        pT[pl.ds(pl.multiple_of(s * rows_in + which * hi, 8), hi), :] = value[:hi]
        pT[pl.ds(pl.multiple_of(cin + s * rows_out + which * ho, 8), ho), :] = value[hi:]

    def to_pair(s):
        return (buf.at[s, other], core_in.at[s], p_send.at[0, s], p_recv.at[0, s], (c, fcore))

    def across(s):
        return (x_out.at[s], x_in.at[s], p_send.at[1, s], p_recv.at[1, s], (c, fx))

    def back(s):
        return (buf.at[s, mine], c_in.at[s], p_send.at[2, s], p_recv.at[2, s], (c, fcore))

    def project(s):
        left = dot1(wi_all[s], hidT[...], NN)
        right = dot1(wo_all[s], goutT[...], NN)
        buf[s, :hi] = left[:hi]
        buf[s, hi:half] = right[:ho]
        buf[s, half : half + hi] = left[hi:]
        buf[s, half + hi :] = right[ho:]
        copy(*to_pair(s)).start()

    def pair_sum(s):
        copy(*to_pair(s)).wait_recv()
        total = buf[s, mine] + core_in[s]
        buf[s, mine] = total
        x_out[s] = total.astype(bf16)
        copy(*across(s)).start()

    def full_sum(s):
        copy(*across(s)).wait_recv()
        total = buf[s, mine] + x_in[s].astype(f32)
        buf[s, mine] = total
        copy(*back(s)).start()
        place(s, core, total)

    def collect(s):
        copy(*back(s)).wait_recv()
        place(s, 1 - core, c_in[s])

    def landed(s, fwd, across_pair):
        for a, (src, dst) in enumerate(both):
            copy(dst.at[s], dst.at[s], g_send.at[2, a, s], g_recv.at[a, s], (yn, f)).wait_recv()
            if fwd is not None:
                has, to, way = fwd
                pl.when(has)(lambda: copy(
                    dst.at[s], dst.at[s], g_send.at[way, a, s], g_recv.at[a, s], (to, f)).start())
            if across_pair:
                copy(dst.at[s], dst.at[s], g_send.at[2, a, s], g_recv.at[a, s], (yn, f)).start()

    def row(k, way):
        there = z - k if way == 0 else z + k
        has = there >= 0 if way == 0 else there < outer
        q = jnp.maximum(there, 0) if way == 0 else jnp.minimum(there, outer - 1)
        fwd = (z < outer - 1, up, 0) if way == 0 else (z > 0, down, 1)
        return has, q, fwd

    events = [(None, c, None, False, False)]
    later = [(None, z * 2 + 1 - y, None, True, False)]
    for k in range(1, outer):
        for way in (0, 1):
            has, q, fwd = row(k, way)
            events.append((has, q * 2 + y, fwd, True, True))
        events.extend(later)
        later = []
        for way in (0, 1):
            has, q, fwd = row(k, way)
            later.append((has, q * 2 + 1 - y, None, True, False))
    events.extend(later)

    def under(has, fn, *args):
        if has is None:
            fn(*args)
        else:
            pl.when(has)(lambda: fn(*args))

    def take(s, fwd, wait, across_pair):
        if wait:
            landed(s, fwd, across_pair)
        project(s)

    def release(s, fwd, across_pair):
        for args in (to_pair(s), across(s), back(s)):
            copy(*args).wait_send()
        for a, (src, dst) in enumerate(both):
            def there(way, to):
                copy(dst.at[s], dst.at[s], g_send.at[way, a, s], g_recv.at[a, s],
                     (to, f)).wait_send()
            if fwd is not None:
                under(fwd[0], there, fwd[2], fwd[1])
            if across_pair:
                there(2, yn)

    total_events = len(events)
    for i in range(total_events + 5):
        if i < total_events:
            has, s, fwd, wait, across_pair = events[i]
            under(has, take, s, fwd, wait, across_pair)
        for lag, fn in ((1, pair_sum), (3, full_sum), (5, collect)):
            if 0 <= i - lag < total_events:
                under(events[i - lag][0], fn, events[i - lag][1])

    e = e_ref[...]
    einv = 1.0 / e
    eend = e[:, tok - 1 : tok]
    gate = pT[:hp, :]
    xs = pT[hp : 2 * hp, :] * einv
    bT = pT[2 * hp : 2 * hp + nst, :]
    cT = pT[2 * hp + nst : cin, :]
    xs2, b2, c2 = split(xs), split(bT), split(cT)
    tmp[...] = dot3(xs2, b2, NT) * eend
    own = pl.ds(pl.multiple_of(f * hpf, 8), hpf)
    st_out[...] = tmp[own, :]
    for k in range(n - 1, 0, -1):
        go(st_out, st_all.at[c], s_send.at[0, k], s_recv.at[0, c],
           (jnp.minimum(c + k, n - 1), f), when=c + k < n)

    upper = lax.broadcasted_iota(jnp.int32, (tok, tok), 0) <= lax.broadcasted_iota(
        jnp.int32, (tok, tok), 1)
    scores2 = split(jnp.where(upper, dot3(transposed(b2), c2, NN), 0.0))
    y_in = dot3(xs2, scores2, NN)
    sig = 1.0 / (1.0 + jnp.exp(-gate))
    silu = gate * sig

    for k in range(1, n):
        s = lax.rem(c + n - k, n)
        arrive(e_out, e_all.at[s], s_send.at[4, k], s_recv.at[4, s], (s, f))
        s = jnp.maximum(c - k, 0)
        arrive(st_out, st_all.at[s], s_send.at[0, k], s_recv.at[0, s], (s, f), when=c - k >= 0)
    state = jnp.zeros((hpf, nst), f32)
    for k in range(n - 1):
        new = e_all[k, 0:1, :] * state + st_all[k]
        state = jnp.where(k < c, new, state)
    s0_ref[own, :] = state
    for k in range(1, fs):
        go(s0_ref.at[own], s0_ref.at[own], s_send.at[1, k], s_recv.at[1, f], (c, lax.rem(f + k, fs)))
    for k in range(1, fs):
        p = lax.rem(f + fs - k, fs)
        rows = pl.ds(pl.multiple_of(p * hpf, 8), hpf)
        copy(s0_ref.at[rows], s0_ref.at[rows], s_send.at[1, k], s_recv.at[1, p], (c, p)).wait_recv()
    s02 = split(s0_ref[...])
    yT = (y_in + dot3(s02, c2, NN)) * e

    gain = gain_ref[...]
    gated = yT * silu
    r = lax.rsqrt(jnp.mean(gated * gated, axis=0, keepdims=True) + EPS)
    normed = (gated * r * gain).astype(bf16)
    u = pT[cin:, :] * gain
    dgated = r * u - gated * (r * r * r * jnp.mean(u * gated, axis=0, keepdims=True))
    dys2 = split(dgated * silu * e)
    tmp[...] = dot3(dys2, c2, NT)
    ad_out[...] = tmp[own, :].astype(bf16)
    for k in range(n - 1, 0, -1):
        go(ad_out, ad_all.at[c], s_send.at[2, k], s_recv.at[2, c],
           (jnp.maximum(c - k, 0), f), when=c - k >= 0)
    gp[:hp, :] = (dgated * yT * (sig * (1.0 + gate * (1.0 - sig)))).astype(bf16)

    ro[...] = dot1(normed, gout_ref[...], NN)
    for q in range(outer):
        at = pl.ds(pl.multiple_of((q * 2 + 1 - y) * rows_out, 8), rows_out)
        ob1[q] = ro[at, :].astype(bf16)
    go(ob1, ob1r, o_send.at[0], o_recv.at[0], (yn, f))

    dscores = jnp.where(upper, dot1(xs2[0].T, dys2[0], NN), 0.0).astype(bf16)
    gp[2 * hp + nst :, :] = (dot1(b2[0], dscores, NN) + dot3(transposed(s02), dys2, NN)).astype(bf16)
    db = dot1(c2[0], dscores, NT)
    dxs = dot1(dys2[0], scores2[0], NT)

    copy(ob1, ob1r, o_send.at[0], o_recv.at[0], (yn, f)).wait_recv()
    for q in range(outer):
        at = pl.ds(pl.multiple_of((q * 2 + y) * rows_out, 8), rows_out)
        total = ro[at, :] + ob1r[q].astype(f32)
        ro[at, :] = total
        ob2[q] = total.astype(bf16)

    for k in range(1, n):
        s = jnp.minimum(c + k, n - 1)
        arrive(ad_out, ad_all.at[s], s_send.at[2, k], s_recv.at[2, s], (s, f), when=c + k < n)
    adj = jnp.zeros((hpf, nst), f32)
    for k in range(n - 1, 0, -1):
        new = e_all[k, 0:1, :] * adj + ad_all[k].astype(f32)
        adj = jnp.where(k > c, new, adj)
    g_ref[own, :] = adj
    for k in range(1, fs):
        go(g_ref.at[own], g_ref.at[own], s_send.at[3, k], s_recv.at[3, f], (c, lax.rem(f + k, fs)))
    for k in range(1, outer):
        q = lax.rem(z + k, outer)
        go(ob2.at[q], ob2r.at[z], o_send.at[k], o_recv.at[1 + z], (q * 2 + y, f))
    for k in range(1, fs):
        p = lax.rem(f + fs - k, fs)
        rows = pl.ds(pl.multiple_of(p * hpf, 8), hpf)
        copy(g_ref.at[rows], g_ref.at[rows], s_send.at[3, k], s_recv.at[3, p], (c, p)).wait_recv()
    g2 = split(g_ref[...] * eend)
    gp[hp : 2 * hp, :] = ((dxs + dot3(g2, b2, NN)) * einv).astype(bf16)
    gp[2 * hp : 2 * hp + nst, :] = (db + dot3(transposed(g2), xs2, NN)).astype(bf16)

    def rows_of(s):
        return pl.ds(pl.multiple_of(s * rows_in, 16), rows_in)

    far = order[::-1] + [0]
    for i, k in enumerate(far):
        q = lax.rem(z + k, outer)
        ib1[i] = dot1(gp[rows_of(q * 2 + 1 - y), :], hid_ref[...], NN).astype(bf16)
        go(ib1.at[i], ib1r.at[i], i_send.at[0, i], i_recv.at[0, i], (yn, f))
    for i, k in enumerate(far):
        q = lax.rem(z + k, outer)
        part = dot1(gp[rows_of(q * 2 + y), :], hid_ref[...], NN)
        copy(ib1.at[i], ib1r.at[i], i_send.at[0, i], i_recv.at[0, i], (yn, f)).wait_recv()
        part = part + ib1r[i].astype(f32)
        if k:
            ib2[i] = part.astype(bf16)
            go(ib2.at[i], ib2r.at[z], i_send.at[1, i], i_recv.at[1, z], (q * 2 + y, f))
        else:
            ri[...] = part

    acc = ro[pl.ds(pl.multiple_of(c * rows_out, 8), rows_out), :]
    for k in range(1, outer):
        q = lax.rem(z + k, outer)
        copy(ob2.at[q], ob2r.at[q], o_send.at[k], o_recv.at[1 + q], (q * 2 + y, f)).wait_recv()
        acc = acc + ob2r[q].astype(f32)
    acc = acc * (1.0 / root_tokens)
    ro[:rows_out, :] = acc
    nout_out[...] = jnp.broadcast_to(jnp.sum(acc * acc, axis=0, keepdims=True), (8, d))
    for k in range(1, n):
        go(nout_out, nout_all.at[c], n_send.at[0, k], n_recv.at[0, c], (lax.rem(c + k, n), f))
    nout_all[c] = nout_out[...]

    gpt = gp[...].T
    wi = wi_all[...].reshape(cin, d)
    gh_ref[...] = dot1(gpt, wi, NN).astype(bf16)

    weight = jnp.zeros((1, d), f32)
    for s in range(n):
        w = wo_all[s].astype(f32)
        weight = weight + jnp.sum(w * w, axis=0, keepdims=True)
    w = win_ref[...].astype(f32)
    weight_in = jnp.sum(w * w, axis=1, keepdims=True)

    acc = ri[...]
    for k in range(1, outer):
        q = lax.rem(z + k, outer)
        copy(ib2.at[0], ib2r.at[q], i_send.at[1, 0], i_recv.at[1, q], (q * 2 + y, f)).wait_recv()
        acc = acc + ib2r[q].astype(f32)
    acc = acc * (1.0 / root_tokens)
    ri[...] = acc
    at = lax.broadcasted_iota(jnp.int32, (rows_in, 128), 1)
    nin_out[...] = jnp.where(at < 64, jnp.sum(acc * acc, axis=1, keepdims=True), weight_in)
    for k in range(1, fs):
        go(nin_out, nin_all.at[f], n_send.at[1, k], n_recv.at[1, f], (c, lax.rem(f + k, fs)))
    nin_all[f] = nin_out[...]

    grad_square = nout_all[c, 0:1, :]
    for k in range(1, n):
        s = lax.rem(c + n - k, n)
        copy(nout_out, nout_all.at[s], n_send.at[0, k], n_recv.at[0, s], (s, f)).wait_recv()
        grad_square = grad_square + nout_all[s, 0:1, :]
    factor = jnp.minimum(1.0, clip_output * jnp.maximum(jnp.sqrt(weight), 0.001)
                         / jnp.maximum(jnp.sqrt(grad_square), 1e-06))
    gwo_ref[...] = ro[:rows_out, :] * factor

    square = nin_all[f]
    for k in range(1, fs):
        p = lax.rem(f + fs - k, fs)
        copy(nin_out, nin_all.at[p], n_send.at[1, k], n_recv.at[1, p], (c, p)).wait_recv()
        square = square + nin_all[p]
    root = jnp.sqrt(square)
    factor = jnp.minimum(1.0, clip_input * jnp.maximum(root[:, 64:65], 0.001)
                         / jnp.maximum(root[:, 0:1], 1e-06))
    gwi_ref[...] = ri[...] * factor
    for has, args in sent:
        under(has, lambda args: copy(*args).wait_send(), args)
    for has, s, fwd, wait, across_pair in events:
        under(has, release, s, fwd, across_pair)


def one_kernel(n, fs, hidden, w_in, decay, norm_gain, w_out, grad_out):
    tok, d = hidden.shape
    rows_in, rows_out = w_in.shape[0], w_out.shape[0]
    cin, hp = rows_in * n, rows_out * n
    nst = (cin - 2 * hp) // 2
    hpf, outer = hp // fs, n // 2
    half = (rows_in + rows_out) // 2
    V = pltpu.VMEM
    dma = pltpu.SemaphoreType.DMA
    scratch = [
        V((d, tok), bf16), V((d, tok), bf16), V((n, rows_in, d), bf16), V((n, rows_out, d), bf16),
        V((cin + hp, tok), f32), V((n, 2 * half, tok), f32), V((n, half, tok), f32),
        V((n, half, tok), bf16), V((n, half, tok), bf16), V((n, half, tok), f32),
        V((8, nst), f32), V((n, 8, nst), f32),
        V((hp, tok), f32), V((hpf, nst), f32), V((n, hpf, nst), f32), V((hp, nst), f32),
        V((hpf, nst), bf16), V((n, hpf, nst), bf16), V((hp, nst), f32),
        V((hp, d), f32), V((outer, rows_out, d), bf16), V((outer, rows_out, d), bf16),
        V((outer, rows_out, d), bf16), V((outer, rows_out, d), bf16),
        V((cin, tok), bf16), V((rows_in, d), f32),
        V((outer, rows_in, d), bf16), V((outer, rows_in, d), bf16),
        V((outer, rows_in, d), bf16), V((outer, rows_in, d), bf16),
        V((rows_in, 128), f32), V((fs, rows_in, 128), f32), V((8, d), f32), V((n, 8, d), f32),
        dma((3, 2, n)), dma((2, n)), dma((3, n)), dma((3, n)), dma((5, n)), dma((5, n)),
        dma((1 + outer,)), dma((1 + outer,)), dma((2, outer)), dma((2, outer)),
        dma((2, n)), dma((2, n)), V((hp, nst), f32),
    ]
    vm = pl.BlockSpec(memory_space=pltpu.VMEM)
    return pl.pallas_call(
        functools.partial(fused, n, fs, math.sqrt(tok * n), math.sqrt(d * fs)),
        out_shape=(
            jax.ShapeDtypeStruct((tok, d), bf16),
            jax.ShapeDtypeStruct((rows_in, d), f32),
            jax.ShapeDtypeStruct((rows_out, d), f32),
        ),
        in_specs=[vm] * 6,
        out_specs=(vm, vm, vm),
        scratch_shapes=scratch,
        compiler_params=pltpu.CompilerParams(
            collective_id=0, has_side_effects=True, vmem_limit_bytes=60 * 1024 * 1024),
    )(hidden, w_in, decay, norm_gain[:, None], w_out, grad_out)


def solution(mesh):
    n, fs = mesh.shape["ctx"], mesh.shape["fsdp"]

    def body(hidden, w_in, decay, norm_gain, w_out, grad_out):
        whole_tiles = w_in.shape[0] % 16 == 0 and w_out.shape[0] % 16 == 0
        if whole_tiles and fs == decay.shape[0] and fs % 2 == 0 and n % 2 == 0 and n >= 4:
            return one_kernel(n, fs, hidden, w_in, decay, norm_gain, w_out, grad_out)
        return local(hidden, w_in, decay, norm_gain, w_out, grad_out)

    return jax.shard_map(
        body,
        mesh=mesh,
        in_specs=(
            P("ctx", "fsdp"),
            P("ctx", "fsdp"),
            P(None, "ctx"),
            P(),
            P("ctx", "fsdp"),
            P("ctx", "fsdp"),
        ),
        out_specs=(P("ctx", "fsdp"), P("ctx", "fsdp"), P("ctx", "fsdp")),
        check_vma=False,
    )
```
